32 devices in a mesh: member: 16 (over z, y, x), tensor: 2 (over core).
Axes of the slice: x: 2, y: 2, z: 4, core: 2. Of those that a mesh axis runs over, the one named last changes fastest.
Arguments:
- tokens: bfloat16 [768, 5120], P('member', 'tensor'), may hold values from -6 to 6
- up_weight: bfloat16 [5120, 27648], P('tensor', 'member'), may hold values from -0.078125 to 0.078125
- left_factors: bfloat16 [192, 5120], P('member', 'tensor'), may hold values from -6 to 6
- right_factors: bfloat16 [192, 27648], P('tensor', 'member'), may hold values from -6 to 6
- fitness: float32 [48], replicated, may hold values from -0.6 to 0.6
Outputs:
- hidden: bfloat16 [768, 27648], P('tensor', 'member')
- gradient: bfloat16 [5120, 27648], P('tensor', 'member')
The draws below stay inside these ranges and needn't reach their ends.
All inputs are finite; a program needn't handle non-finite values.
Results may differ from the reference program's by a relative error of at most 0.014.
Values may be sent and summed in bfloat16 or wider, within the bound.
A program may use at most 64 MiB of HBM per device.

```python
import jax
import jax.numpy as jnp

D = 5120
FFN_HIDDEN = 27648
RANK = 4
MEMBER_TOKENS = 16
POPULATION_SIZE = 48
TOKEN_TOTAL = 768
N_TENSOR = 2


def shard_levels(key, dims, cuts, least, high):
    loudness = 1.0
    for dim, shards_of in cuts:
        heights = jax.random.uniform(jax.random.fold_in(jax.random.fold_in(key, 6), dim), (shards_of,), jnp.float32, least / len(cuts), high / len(cuts))
        loudness = loudness * jnp.repeat(jnp.exp(heights), dims[dim] // shards_of).reshape((-1,) + (1,) * (len(dims) - 1 - dim))
    return loudness


def gaussian(own_key, dims, width, limit, pieces=(), held_as=jnp.bfloat16):
    drawn = width * jax.random.normal(own_key, dims, jnp.float32)
    if pieces:
        drawn = drawn * shard_levels(own_key, dims, pieces, -0.22, 0.18)
    return jnp.clip(drawn, -limit, limit).astype(held_as)


def setup_inputs(seed: int = 0) -> dict:
    key_of = jax.random.split(jax.random.key(seed), 6)
    return {
        "tokens": gaussian(key_of[0], (TOKEN_TOTAL, D), 1.0, 6.0, ((0, 16), (1, 2))),
        "up_weight": gaussian(key_of[1], (D, FFN_HIDDEN), D ** -0.5, 0.078125, ((0, 2), (1, 16))),
        "left_factors": gaussian(key_of[2], (POPULATION_SIZE * RANK, D), 1.0, 6.0, ((0, 16), (1, 2))),
        "right_factors": gaussian(key_of[3], (POPULATION_SIZE * RANK, FFN_HIDDEN), 1.0, 6.0, ((0, 2), (1, 16))),
        "fitness": gaussian(key_of[4], (POPULATION_SIZE,), 0.1, 0.6, (), jnp.float32),
    }


def reference(tokens, up_weight, left_factors, right_factors, fitness):
    noise_scale = 0.25 * D ** -0.5
    mixing = noise_scale * RANK ** -0.5
    block_span_width = D // N_TENSOR
    right_factor_wide = right_factors.astype(jnp.float32).reshape(POPULATION_SIZE, RANK, FFN_HIDDEN)
    hidden_sum = jnp.zeros((TOKEN_TOTAL, FFN_HIDDEN), jnp.float32)
    for tensor_block in range(N_TENSOR):
        lower = tensor_block * block_span_width
        token_columns = tokens[:, lower:lower + block_span_width]
        left_cols = left_factors[:, lower:lower + block_span_width]
        base_term = jnp.dot(token_columns, up_weight[lower:lower + block_span_width, :], preferred_element_type=jnp.float32)
        up_projection = jnp.einsum("uzg,uig->uzi", token_columns.astype(jnp.float32).reshape(POPULATION_SIZE, MEMBER_TOKENS, block_span_width),
                                left_cols.astype(jnp.float32).reshape(POPULATION_SIZE, RANK, block_span_width)).astype(jnp.bfloat16)
        lowrank_correction = jnp.einsum("djt,dty->djy", up_projection.astype(jnp.float32), right_factor_wide).reshape(TOKEN_TOTAL, FFN_HIDDEN)
        partial_value = (base_term + mixing * lowrank_correction).astype(jnp.bfloat16)
        hidden_sum = hidden_sum + partial_value.astype(jnp.float32)
    hidden = hidden_sum.astype(jnp.bfloat16)
    fit_rows = jnp.repeat(fitness, RANK)
    weighted = (fit_rows[:, None] * left_factors.astype(jnp.float32)).astype(jnp.bfloat16)
    gradient = jnp.dot(weighted.T, right_factors, preferred_element_type=jnp.float32)
    gradient = gradient * (1.0 / (POPULATION_SIZE * noise_scale * RANK ** 0.5))
    return hidden, gradient.astype(jnp.bfloat16)
```

```python
import functools

import jax
import jax.numpy as jnp
from jax import lax
from jax.experimental import pallas as pl
from jax.experimental.pallas import tpu as pltpu
from jax.sharding import PartitionSpec as P

D = 5120
RANK = 4
MEMBER_TOKENS = 16
MESH = pl.DeviceIdType.MESH
NT = (((1,), (1,)), ((), ()))
TN = (((0,), (0,)), ((), ()))


def plain_body(tokens, up_weight, left_factors, right_factors, fitness):
    noise_scale = 0.25 * D ** (-0.5)
    mixing = noise_scale * RANK ** (-0.5)
    width = tokens.shape[1]
    columns = up_weight.shape[1]
    right_all = lax.all_gather(right_factors, "tensor", axis=0, tiled=True)
    members = right_all.shape[0] // RANK
    left_all = lax.all_gather(left_factors, "member", axis=0, tiled=True)
    all_tokens = lax.all_gather(tokens, "member", axis=0, tiled=True)
    projection = jnp.einsum(
        "uzg,uig->uzi",
        all_tokens.reshape(members, MEMBER_TOKENS, width),
        left_all.reshape(members, RANK, width),
        preferred_element_type=jnp.float32,
    ).astype(jnp.bfloat16)
    base = jnp.dot(all_tokens, up_weight, preferred_element_type=jnp.float32)
    correction = jnp.einsum(
        "djt,dty->djy",
        projection,
        right_all.reshape(members, RANK, columns),
        preferred_element_type=jnp.float32,
    ).reshape(base.shape)
    summed = lax.psum_scatter(
        (base + mixing * correction).astype(jnp.bfloat16), "tensor", scatter_dimension=0, tiled=True
    )
    fit_rows = jnp.repeat(fitness, RANK)
    weighted = (fit_rows[:, None] * left_all.astype(jnp.float32)).astype(jnp.bfloat16)
    gradient = jnp.einsum("kd,kf->df", weighted, right_all, preferred_element_type=jnp.float32)
    gradient = gradient * (1.0 / (members * noise_scale * RANK**0.5))
    return (summed, gradient.astype(jnp.bfloat16))


def mirror(steps):
    turn = {"u": "v", "v": "u", "x": "x", "y": "y"}
    return [
        ([(k, 3 - l) for k, l in waits], [((k, 3 - l), turn[d]) for (k, l), d in sends])
        for waits, sends in steps
    ]


def halves(l):
    return ([("x", l), ("y", l)], [(("x", l), "y"), (("y", l), "x")])


def on(l, dirs):
    return ([("c", l)], [(("c", l), d) for d in dirs])


END = [
    [halves(0), on(1, "xy"), ([("d", 0)], [(("d", 0), "u")])],
    [on(2, "xy"), on(3, "xy"), ([("x", 1), ("y", 1), ("D", 1)], [])],
    [halves(3), ([("x", 2), ("y", 2), ("D", 2)], [])],
    [([("d", 3)], [])],
]
MID = [
    [halves(1), on(0, "uxy"), on(2, "vxy"), ([("d", 1)], [])],
    [on(3, "vxy"), ([], [(("d", 1), "v"), (("d", 1), "u")]), ([("x", 0), ("y", 0), ("D", 0)], [])],
    [([("x", 2), ("y", 2)], []), ([("D", 2)], [(("D", 2), "v")]), halves(3)],
    [([("d", 3)], [])],
]
PLAN = [END, MID, [mirror(s) for s in MID], [mirror(s) for s in END]]
ORDER = [[0, 1, 2, 3], [1, 0, 2, 3], [2, 3, 1, 0], [3, 2, 1, 0]]


def tile_of(n, step, most):
    best = step
    for size in range(step, most + 1, step):
        if n % size == 0:
            best = size
    return best


def gather_kernel(
    mixing, tok_in, w_in, left_in, right_in,
    rt_ref, lpad_ref, own_ref, got_ref,
    tok, left, w, rall, sendb,
    send_sem, recv_sem, local_sem, w_sem, r_send, r_recv, p_send, p_recv,
):
    m = lax.axis_index("member")
    t = lax.axis_index("tensor")
    z, y, x = m // 4, (m // 2) % 2, m % 2
    width = tok_in.shape[1]
    half = width // 2
    rows = tok_in.shape[0]
    pad = lpad_ref.shape[0] // 16
    facts = left_in.shape[0]
    ftotal = w.shape[0]

    def at(l, yy, xx):
        return 4 * l + 2 * yy + xx

    def member_of(kind, l):
        if kind == "c":
            return at(l, y, x)
        if kind == "x":
            return at(l, y, 1 - x)
        if kind == "y":
            return at(l, 1 - y, x)
        return at(l, 1 - y, 1 - x)

    barrier = pltpu.get_barrier_semaphore()
    for peer in (at(z, y, 1 - x), at(z, 1 - y, x)):
        pl.semaphore_signal(barrier, inc=1, device_id=(peer, t), device_id_type=MESH)
    pl.semaphore_signal(barrier, inc=1, device_id=(m, 1 - t), device_id_type=MESH)

    @pl.when(z > 0)
    def _():
        pl.semaphore_signal(barrier, inc=1, device_id=(m - 4, t), device_id_type=MESH)

    @pl.when(z < 3)
    def _():
        pl.semaphore_signal(barrier, inc=1, device_id=(m + 4, t), device_id_type=MESH)

    local = [
        pltpu.make_async_copy(tok_in, tok.at[m], local_sem.at[0]),
        pltpu.make_async_copy(left_in, left.at[m], local_sem.at[1]),
        pltpu.make_async_copy(right_in, rall.at[t], local_sem.at[2]),
        pltpu.make_async_copy(w_in, w, w_sem),
    ]
    for copy in local:
        copy.start()

    @pl.when((z == 0) | (z == 3))
    def _():
        pl.semaphore_wait(barrier, 4)

    @pl.when((z == 1) | (z == 2))
    def _():
        pl.semaphore_wait(barrier, 5)

    bufs = (tok, left)

    def peer_of(direction, plane):
        if direction == "x":
            return at(plane, y, 1 - x)
        if direction == "y":
            return at(plane, 1 - y, x)
        return at(plane + (1 if direction == "u" else -1), y, x)

    def copies(item, direction, plane, slot):
        kind, l = item
        own = kind == "c" and l == plane
        who = member_of(kind, l)
        out = []
        cut = kind in "xy"
        part = 0 if direction == "y" else 1
        for b, buf in enumerate(bufs):
            src = (tok_in, left_in)[b] if own else buf.at[who]
            dst = buf.at[who]
            if cut:
                src = src.at[:, pl.ds(part * half, half)]
                dst = dst.at[:, pl.ds(part * half, half)]
            out.append(
                pltpu.make_async_remote_copy(
                    src_ref=src,
                    dst_ref=dst,
                    send_sem=send_sem.at[b, slot],
                    recv_sem=recv_sem.at[b, who, part if cut else 0],
                    device_id=(peer_of(direction, plane), t),
                    device_id_type=MESH,
                )
            )
        return out

    def await_item(item):
        kind, l = item
        who = member_of(kind, l)
        for b, buf in enumerate(bufs):
            if kind == "d":
                for part in range(2):
                    piece = buf.at[who, :, pl.ds(part * half, half)]
                    pltpu.make_async_copy(piece, piece, recv_sem.at[b, who, part]).wait()
            else:
                pltpu.make_async_copy(buf.at[who], buf.at[who], recv_sem.at[b, who, 0]).wait()

    started = {k: [] for k in range(4)}

    def send(item, direction, plane):
        pair = copies(item, direction, plane, len(started[plane]))
        started[plane].append((item, direction))
        for copy in pair:
            copy.start()

    for plane in range(4):
        @pl.when(z == plane)
        def _(plane=plane):
            dirs = {0: "uxy", 3: "vxy"}.get(plane, "uvxy")
            for d in dirs:
                send(("c", plane), d, plane)

    r_copy = pltpu.make_async_remote_copy(
        src_ref=right_in, dst_ref=rall.at[t], send_sem=r_send, recv_sem=r_recv,
        device_id=(m, 1 - t), device_id_type=MESH,
    )
    r_copy.start()

    lpad_ref[...] = jnp.zeros_like(lpad_ref)
    kk = lax.broadcasted_iota(jnp.int32, (2 * rall.shape[1], 16 * pad), 0)
    qq = lax.broadcasted_iota(jnp.int32, (2 * rall.shape[1], 16 * pad), 1)
    slot_q = qq % pad
    spread = jnp.where((slot_q < facts) & (kk == facts * (qq // pad) + slot_q), 1.0, 0.0)
    spread = spread.astype(jnp.bfloat16)
    local[2].wait()
    r_copy.wait()
    r_val = jnp.concatenate([rall[0], rall[1]], axis=0)
    rt_ref[...] = lax.dot_general(
        r_val, spread, TN, preferred_element_type=jnp.float32
    ).astype(jnp.bfloat16)
    local[0].wait()
    local[1].wait()

    ft = tile_of(ftotal, 16, 448)

    def layer_index(step):
        ind = 0
        for plane in range(4):
            ind = ind + jnp.where(z == plane, ORDER[plane][step], 0)
        return ind

    def compute(l, out_ref):
        side = l % 2
        for i in range(4):
            lv = left[4 * l + i]
            if facts < pad:
                lv = jnp.concatenate([lv, jnp.zeros((pad - facts, width), lv.dtype)], axis=0)
            lpad_ref[pl.ds(pl.multiple_of((4 * l + i) * pad, 16), pad), :] = lv
        toks = tok[pl.ds(4 * l, 4)].reshape(4 * rows, width)
        proj = lax.dot_general(toks, lpad_ref[...], NT, preferred_element_type=jnp.float32)
        rr = lax.broadcasted_iota(jnp.int32, proj.shape, 0)
        qc = lax.broadcasted_iota(jnp.int32, proj.shape, 1)
        sq = qc % pad
        mine = (sq < facts) & (
            (facts // RANK) * (qc // pad) + sq // RANK == (4 * rows // MEMBER_TOKENS) * l + rr // MEMBER_TOKENS
        )
        proj = jnp.where(mine, proj, 0.0).astype(jnp.bfloat16)

        @pl.loop(0, ftotal // ft)
        def _(i):
            span = pl.ds(pl.multiple_of(i * ft, 16), ft)
            value = lax.dot_general(
                w[span, :], tok[pl.ds(4 * l, 4)].reshape(4 * rows, width), NT,
                preferred_element_type=jnp.float32,
            )
            value = value + mixing * lax.dot_general(
                rt_ref[span, :], proj, NT, preferred_element_type=jnp.float32
            )
            out_ref[side, span, :] = value.astype(jnp.bfloat16)

    def exchange(side):
        return pltpu.make_async_remote_copy(
            src_ref=sendb.at[side], dst_ref=got_ref.at[side],
            send_sem=p_send.at[side], recv_sem=p_recv.at[side],
            device_id=(m, 1 - t), device_id_type=MESH,
        )

    for step in range(4):
        for plane in range(4):
            @pl.when(z == plane)
            def _(plane=plane, step=step):
                for waits, sends in PLAN[plane][step]:
                    for item in waits:
                        await_item(item)
                    for item, d in sends:
                        send(item, d, plane)
        l = layer_index(step)
        if step == 0:
            local[3].wait()

        @pl.when(l // 2 == t)
        def _():
            compute(l, own_ref)

        @pl.when(l // 2 != t)
        def _():
            compute(l, sendb)
            exchange(l % 2).start()

    for plane in range(4):
        @pl.when(z == plane)
        def _(plane=plane):
            for slot, (item, d) in enumerate(started[plane]):
                for copy in copies(item, d, plane, slot):
                    copy.wait_send()
    for side in range(2):
        exchange(side).wait()


def finish_kernel(scale, facts, fit_ref, lpad_ref, rt_ref, own_ref, got_ref, h_ref, g_ref, wl):
    pad = wl.shape[0] // 16

    @pl.when(pl.program_id(0) == 0)
    def _():
        for b in range(16):
            rows = lax.broadcasted_iota(jnp.int32, (pad, 1), 0) // RANK
            col = jnp.zeros((pad, 1), jnp.float32)
            for j in range(facts // RANK):
                col = jnp.where(rows == j, fit_ref[b * (facts // RANK) + j], col)
            part = lpad_ref[pl.ds(b * pad, pad), :].astype(jnp.float32) * col
            wl[pl.ds(b * pad, pad), :] = part.astype(jnp.bfloat16)

    n = own_ref.shape[2]
    for side in range(2):
        total = own_ref[side].astype(jnp.float32) + got_ref[side].astype(jnp.float32)
        h_ref[:, side * n:(side + 1) * n] = total.astype(jnp.bfloat16)
    g = jnp.dot(rt_ref[...], wl[...], preferred_element_type=jnp.float32)
    g_ref[...] = (g * scale).astype(jnp.bfloat16)


def body(tokens, up_weight, left_factors, right_factors, fitness):
    noise_scale = 0.25 * D ** (-0.5)
    mixing = noise_scale * RANK ** (-0.5)
    rows, width = tokens.shape
    facts = left_factors.shape[0]
    columns = up_weight.shape[1]
    rrows = right_factors.shape[0]
    pad = -(-facts // 16) * 16
    members = fitness.shape[0]
    bf = jnp.bfloat16
    anyspec = pl.BlockSpec(memory_space=pl.ANY)
    vm = pl.BlockSpec(memory_space=pltpu.VMEM)
    dma = pltpu.SemaphoreType.DMA
    nsend = 24
    part = jax.ShapeDtypeStruct((2, columns, 4 * rows), bf)
    rt, lpad, own, got = pl.pallas_call(
        functools.partial(gather_kernel, mixing),
        out_shape=(
            jax.ShapeDtypeStruct((columns, 16 * pad), bf),
            jax.ShapeDtypeStruct((16 * pad, width), bf),
            part,
            part,
        ),
        in_specs=[anyspec] * 4,
        out_specs=(vm, vm, vm, vm),
        scratch_shapes=[
            pltpu.VMEM((16, rows, width), bf),
            pltpu.VMEM((16, facts, width), bf),
            pltpu.VMEM((columns, width), bf),
            pltpu.VMEM((2, rrows, columns), bf),
            pltpu.VMEM((2, columns, 4 * rows), bf),
            dma((2, nsend)), dma((2, 16, 2)), dma((3,)), dma, dma, dma, dma((2,)), dma((2,)),
        ],
        compiler_params=pltpu.CompilerParams(
            collective_id=0, has_side_effects=True, vmem_limit_bytes=40 * 1024 * 1024
        ),
        name="gather_project",
    )(tokens, up_weight.T, left_factors, right_factors)

    tf = tile_of(columns, 16, 192)
    hidden, gradient = pl.pallas_call(
        functools.partial(finish_kernel, 1.0 / (members * noise_scale * RANK**0.5), facts),
        grid=(columns // tf,),
        out_shape=(
            jax.ShapeDtypeStruct((columns, 8 * rows), bf),
            jax.ShapeDtypeStruct((columns, width), bf),
        ),
        in_specs=[
            pl.BlockSpec(memory_space=pltpu.SMEM),
            pl.BlockSpec((16 * pad, width), lambda i: (0, 0)),
            pl.BlockSpec((tf, 16 * pad), lambda i: (i, 0)),
            pl.BlockSpec((2, tf, 4 * rows), lambda i: (0, i, 0)),
            pl.BlockSpec((2, tf, 4 * rows), lambda i: (0, i, 0)),
        ],
        out_specs=(
            pl.BlockSpec((tf, 8 * rows), lambda i: (i, 0)),
            pl.BlockSpec((tf, width), lambda i: (i, 0)),
        ),
        scratch_shapes=[pltpu.VMEM((16 * pad, width), bf)],
        compiler_params=pltpu.CompilerParams(vmem_limit_bytes=24 * 1024 * 1024),
        name="finish",
    )(fitness, lpad, rt, own, got)
    return hidden.T, gradient.T


def solution(mesh):
    fits = mesh.shape["member"] == 16 and mesh.shape["tensor"] == 2
    return jax.shard_map(
        body if fits else plain_body,
        mesh=mesh,
        in_specs=(
            P("member", "tensor"),
            P("tensor", "member"),
            P("member", "tensor"),
            P("tensor", "member"),
            P(),
        ),
        out_specs=(P("tensor", "member"), P("tensor", "member")),
        check_vma=False,
    )
```

```python
import functools

import jax
import jax.numpy as jnp
from jax import lax
from jax.experimental import pallas as pl
from jax.experimental.pallas import tpu as pltpu
from jax.sharding import PartitionSpec as P

D = 5120
RANK = 4
MEMBER_TOKENS = 16
MESH = pl.DeviceIdType.MESH
NT = (((1,), (1,)), ((), ()))
TN = (((0,), (0,)), ((), ()))


def plain_body(tokens, up_weight, left_factors, right_factors, fitness):
    noise_scale = 0.25 * D ** (-0.5)
    mixing = noise_scale * RANK ** (-0.5)
    width = tokens.shape[1]
    columns = up_weight.shape[1]
    right_all = lax.all_gather(right_factors, "tensor", axis=0, tiled=True)
    members = right_all.shape[0] // RANK
    left_all = lax.all_gather(left_factors, "member", axis=0, tiled=True)
    all_tokens = lax.all_gather(tokens, "member", axis=0, tiled=True)
    projection = jnp.einsum(
        "uzg,uig->uzi",
        all_tokens.reshape(members, MEMBER_TOKENS, width),
        left_all.reshape(members, RANK, width),
        preferred_element_type=jnp.float32,
    ).astype(jnp.bfloat16)
    base = jnp.dot(all_tokens, up_weight, preferred_element_type=jnp.float32)
    correction = jnp.einsum(
        "djt,dty->djy",
        projection,
        right_all.reshape(members, RANK, columns),
        preferred_element_type=jnp.float32,
    ).reshape(base.shape)
    summed = lax.psum_scatter(
        (base + mixing * correction).astype(jnp.bfloat16), "tensor", scatter_dimension=0, tiled=True
    )
    fit_rows = jnp.repeat(fitness, RANK)
    weighted = (fit_rows[:, None] * left_all.astype(jnp.float32)).astype(jnp.bfloat16)
    gradient = jnp.einsum("kd,kf->df", weighted, right_all, preferred_element_type=jnp.float32)
    gradient = gradient * (1.0 / (members * noise_scale * RANK**0.5))
    return (summed, gradient.astype(jnp.bfloat16))


def mirror(steps):
    turn = {"u": "v", "v": "u", "x": "x", "y": "y"}
    return [
        ([(k, 3 - l) for k, l in waits], [((k, 3 - l), turn[d]) for (k, l), d in sends])
        for waits, sends in steps
    ]


def halves(l):
    return ([("x", l), ("y", l)], [(("x", l), "y"), (("y", l), "x")])


def on(l, dirs):
    return ([("c", l)], [(("c", l), d) for d in dirs])


END = [
    [halves(0), on(1, "xy"), ([("d", 0)], [(("d", 0), "u")])],
    [on(2, "xy"), ([("x", 1), ("y", 1), ("D", 1)], [])],
    [halves(2), on(3, "xy"), ([("d", 2)], [])],
    [([("x", 3), ("y", 3), ("D", 3)], [])],
]
MID = [
    [halves(1), on(0, "uxy"), on(2, "vxy"), ([("d", 1)], [(("d", 1), "v")])],
    [on(3, "v"), ([("x", 0), ("y", 0), ("D", 0)], [(("D", 0), "u")])],
    [halves(2), ([], [(("c", 3), "x"), (("c", 3), "y")]), ([("D", 3)], [(("D", 3), "v")]), ([("d", 2)], [])],
    [([("x", 3), ("y", 3)], [])],
]
PLAN = [END, MID, [mirror(s) for s in MID], [mirror(s) for s in END]]
ORDER = [[0, 1, 2, 3], [1, 0, 2, 3], [2, 3, 1, 0], [3, 2, 1, 0]]


def tile_of(n, step, most):
    best = step
    for size in range(step, most + 1, step):
        if n % size == 0:
            best = size
    return best


def gather_kernel(
    mixing, tok_in, w_in, left_in, right_in,
    rt_ref, lpad_ref, own_ref, got_ref,
    tok, left, w, rall, sendb,
    send_sem, recv_sem, local_sem, w_sem, r_send, r_recv, p_send, p_recv,
):
    m = lax.axis_index("member")
    t = lax.axis_index("tensor")
    z, y, x = m // 4, (m // 2) % 2, m % 2
    width = tok_in.shape[1]
    half = width // 2
    rows = tok_in.shape[0]
    pad = lpad_ref.shape[0] // 16
    facts = left_in.shape[0]
    ftotal = w.shape[0]

    def at(l, yy, xx):
        return 4 * l + 2 * yy + xx

    def member_of(kind, l):
        if kind == "c":
            return at(l, y, x)
        if kind == "x":
            return at(l, y, 1 - x)
        if kind == "y":
            return at(l, 1 - y, x)
        return at(l, 1 - y, 1 - x)

    barrier = pltpu.get_barrier_semaphore()
    for peer in (at(z, y, 1 - x), at(z, 1 - y, x)):
        pl.semaphore_signal(barrier, inc=1, device_id=(peer, t), device_id_type=MESH)
    pl.semaphore_signal(barrier, inc=1, device_id=(m, 1 - t), device_id_type=MESH)

    @pl.when(z > 0)
    def _():
        pl.semaphore_signal(barrier, inc=1, device_id=(m - 4, t), device_id_type=MESH)

    @pl.when(z < 3)
    def _():
        pl.semaphore_signal(barrier, inc=1, device_id=(m + 4, t), device_id_type=MESH)

    local = [
        pltpu.make_async_copy(tok_in, tok.at[m], local_sem.at[0]),
        pltpu.make_async_copy(left_in, left.at[m], local_sem.at[1]),
        pltpu.make_async_copy(right_in, rall.at[t], local_sem.at[2]),
        pltpu.make_async_copy(w_in, w, w_sem),
    ]
    for copy in local:
        copy.start()

    @pl.when((z == 0) | (z == 3))
    def _():
        pl.semaphore_wait(barrier, 4)

    @pl.when((z == 1) | (z == 2))
    def _():
        pl.semaphore_wait(barrier, 5)

    bufs = (tok, left)

    def peer_of(direction, plane):
        if direction == "x":
            return at(plane, y, 1 - x)
        if direction == "y":
            return at(plane, 1 - y, x)
        return at(plane + (1 if direction == "u" else -1), y, x)

    def copies(item, direction, plane, slot):
        kind, l = item
        own = kind == "c" and l == plane
        who = member_of(kind, l)
        out = []
        cut = kind in "xy"
        part = 0 if direction == "y" else 1
        for b, buf in enumerate(bufs):
            src = (tok_in, left_in)[b] if own else buf.at[who]
            dst = buf.at[who]
            if cut:
                src = src.at[:, pl.ds(part * half, half)]
                dst = dst.at[:, pl.ds(part * half, half)]
            out.append(
                pltpu.make_async_remote_copy(
                    src_ref=src,
                    dst_ref=dst,
                    send_sem=send_sem.at[b, slot],
                    recv_sem=recv_sem.at[b, who, part if cut else 0],
                    device_id=(peer_of(direction, plane), t),
                    device_id_type=MESH,
                )
            )
        return out

    def await_item(item):
        kind, l = item
        who = member_of(kind, l)
        for b, buf in enumerate(bufs):
            if kind == "d":
                for part in range(2):
                    piece = buf.at[who, :, pl.ds(part * half, half)]
                    pltpu.make_async_copy(piece, piece, recv_sem.at[b, who, part]).wait()
            else:
                pltpu.make_async_copy(buf.at[who], buf.at[who], recv_sem.at[b, who, 0]).wait()

    started = {k: [] for k in range(4)}

    def send(item, direction, plane):
        pair = copies(item, direction, plane, len(started[plane]))
        started[plane].append((item, direction))
        for copy in pair:
            copy.start()

    for plane in range(4):
        @pl.when(z == plane)
        def _(plane=plane):
            dirs = {0: "uxy", 3: "vxy"}.get(plane, "uvxy")
            for d in dirs:
                send(("c", plane), d, plane)

    r_copy = pltpu.make_async_remote_copy(
        src_ref=right_in, dst_ref=rall.at[t], send_sem=r_send, recv_sem=r_recv,
        device_id=(m, 1 - t), device_id_type=MESH,
    )
    r_copy.start()

    lpad_ref[...] = jnp.zeros_like(lpad_ref)
    kk = lax.broadcasted_iota(jnp.int32, (2 * rall.shape[1], 16 * pad), 0)
    qq = lax.broadcasted_iota(jnp.int32, (2 * rall.shape[1], 16 * pad), 1)
    slot_q = qq % pad
    spread = jnp.where((slot_q < facts) & (kk == facts * (qq // pad) + slot_q), 1.0, 0.0)
    spread = spread.astype(jnp.bfloat16)
    local[2].wait()
    r_copy.wait()
    r_val = jnp.concatenate([rall[0], rall[1]], axis=0)
    rt_ref[...] = lax.dot_general(
        r_val, spread, TN, preferred_element_type=jnp.float32
    ).astype(jnp.bfloat16)
    local[0].wait()
    local[1].wait()

    ft = tile_of(ftotal, 16, 448)

    def layer_index(step):
        ind = 0
        for plane in range(4):
            ind = ind + jnp.where(z == plane, ORDER[plane][step], 0)
        return ind

    def compute(l, out_ref):
        side = l % 2
        for i in range(4):
            lv = left[4 * l + i]
            if facts < pad:
                lv = jnp.concatenate([lv, jnp.zeros((pad - facts, width), lv.dtype)], axis=0)
            lpad_ref[pl.ds(pl.multiple_of((4 * l + i) * pad, 16), pad), :] = lv
        toks = tok[pl.ds(4 * l, 4)].reshape(4 * rows, width)
        proj = lax.dot_general(toks, lpad_ref[...], NT, preferred_element_type=jnp.float32)
        rr = lax.broadcasted_iota(jnp.int32, proj.shape, 0)
        qc = lax.broadcasted_iota(jnp.int32, proj.shape, 1)
        sq = qc % pad
        mine = (sq < facts) & (
            (facts // RANK) * (qc // pad) + sq // RANK == (4 * rows // MEMBER_TOKENS) * l + rr // MEMBER_TOKENS
        )
        proj = jnp.where(mine, proj, 0.0).astype(jnp.bfloat16)

        @pl.loop(0, ftotal // ft)
        def _(i):
            span = pl.ds(pl.multiple_of(i * ft, 16), ft)
            value = lax.dot_general(
                w[span, :], tok[pl.ds(4 * l, 4)].reshape(4 * rows, width), NT,
                preferred_element_type=jnp.float32,
            )
            value = value + mixing * lax.dot_general(
                rt_ref[span, :], proj, NT, preferred_element_type=jnp.float32
            )
            out_ref[side, span, :] = value.astype(jnp.bfloat16)

    def exchange(side):
        return pltpu.make_async_remote_copy(
            src_ref=sendb.at[side], dst_ref=got_ref.at[side],
            send_sem=p_send.at[side], recv_sem=p_recv.at[side],
            device_id=(m, 1 - t), device_id_type=MESH,
        )

    for step in range(4):
        for plane in range(4):
            @pl.when(z == plane)
            def _(plane=plane, step=step):
                for waits, sends in PLAN[plane][step]:
                    for item in waits:
                        await_item(item)
                    for item, d in sends:
                        send(item, d, plane)
        l = layer_index(step)
        if step == 0:
            local[3].wait()

        @pl.when(l // 2 == t)
        def _():
            compute(l, own_ref)

        @pl.when(l // 2 != t)
        def _():
            compute(l, sendb)
            exchange(l % 2).start()

    for plane in range(4):
        @pl.when(z == plane)
        def _(plane=plane):
            for slot, (item, d) in enumerate(started[plane]):
                for copy in copies(item, d, plane, slot):
                    copy.wait_send()
    for side in range(2):
        exchange(side).wait()


def finish_kernel(scale, facts, fit_ref, lpad_ref, rt_ref, own_ref, got_ref, h_ref, g_ref):
    pad = lpad_ref.shape[0] // 16
    rows = lax.broadcasted_iota(jnp.int32, (pad, 1), 0) // RANK
    parts = []
    for b in range(16):
        col = jnp.zeros((pad, 1), jnp.float32)
        for j in range(facts // RANK):
            col = jnp.where(rows == j, fit_ref[b * (facts // RANK) + j], col)
        parts.append((lpad_ref[pl.ds(b * pad, pad), :].astype(jnp.float32) * col).astype(jnp.bfloat16))
    g = jnp.dot(rt_ref[...], jnp.concatenate(parts, axis=0), preferred_element_type=jnp.float32)
    g_ref[...] = (g * scale).astype(jnp.bfloat16)
    n = own_ref.shape[2]
    for side in range(2):
        total = own_ref[side].astype(jnp.float32) + got_ref[side].astype(jnp.float32)
        h_ref[:, side * n:(side + 1) * n] = total.astype(jnp.bfloat16)


def body(tokens, up_weight, left_factors, right_factors, fitness):
    noise_scale = 0.25 * D ** (-0.5)
    mixing = noise_scale * RANK ** (-0.5)
    rows, width = tokens.shape
    facts = left_factors.shape[0]
    columns = up_weight.shape[1]
    rrows = right_factors.shape[0]
    pad = -(-facts // 16) * 16
    members = fitness.shape[0]
    bf = jnp.bfloat16
    anyspec = pl.BlockSpec(memory_space=pltpu.HBM)
    vm = pl.BlockSpec(memory_space=pltpu.VMEM)
    dma = pltpu.SemaphoreType.DMA
    nsend = 24
    part = jax.ShapeDtypeStruct((2, columns, 4 * rows), bf)
    rt, lpad, own, got = pl.pallas_call(
        functools.partial(gather_kernel, mixing),
        out_shape=(
            jax.ShapeDtypeStruct((columns, 16 * pad), bf),
            jax.ShapeDtypeStruct((16 * pad, width), bf),
            part,
            part,
        ),
        in_specs=[anyspec] * 4,
        out_specs=(vm, vm, vm, vm),
        scratch_shapes=[
            pltpu.VMEM((16, rows, width), bf),
            pltpu.VMEM((16, facts, width), bf),
            pltpu.VMEM((columns, width), bf),
            pltpu.VMEM((2, rrows, columns), bf),
            pltpu.VMEM((2, columns, 4 * rows), bf),
            dma((2, nsend)), dma((2, 16, 2)), dma((3,)), dma, dma, dma, dma((2,)), dma((2,)),
        ],
        compiler_params=pltpu.CompilerParams(
            collective_id=0, has_side_effects=True, vmem_limit_bytes=40 * 1024 * 1024
        ),
        name="gather_project",
    )(
        pltpu.with_memory_space_constraint(tokens, pltpu.HBM),
        pltpu.with_memory_space_constraint(up_weight.T, pltpu.HBM),
        pltpu.with_memory_space_constraint(left_factors, pltpu.HBM),
        pltpu.with_memory_space_constraint(right_factors, pltpu.HBM),
    )

    tf = tile_of(columns, 16, 192)
    td = tile_of(width, 128, 256)
    steps = max(width // td, columns // tf)
    last_f, last_d = columns // tf - 1, width // td - 1
    hidden, gradient = pl.pallas_call(
        functools.partial(finish_kernel, 1.0 / (members * noise_scale * RANK**0.5), facts),
        grid=(steps,),
        out_shape=(
            jax.ShapeDtypeStruct((columns, 8 * rows), bf),
            jax.ShapeDtypeStruct((columns, width), bf),
        ),
        in_specs=[
            pl.BlockSpec(memory_space=pltpu.SMEM),
            pl.BlockSpec((16 * pad, td), lambda i: (0, jnp.minimum(i, last_d))),
            pl.BlockSpec((columns, 16 * pad), lambda i: (0, 0)),
            pl.BlockSpec((2, tf, 4 * rows), lambda i: (0, jnp.minimum(i, last_f), 0)),
            pl.BlockSpec((2, tf, 4 * rows), lambda i: (0, jnp.minimum(i, last_f), 0)),
        ],
        out_specs=(
            pl.BlockSpec((tf, 8 * rows), lambda i: (jnp.minimum(i, last_f), 0)),
            pl.BlockSpec((columns, td), lambda i: (0, jnp.minimum(i, last_d))),
        ),
        compiler_params=pltpu.CompilerParams(vmem_limit_bytes=24 * 1024 * 1024),
        name="finish",
    )(fitness, lpad, rt, own, got)
    return hidden.T, gradient.T


def solution(mesh):
    fits = mesh.shape["member"] == 16 and mesh.shape["tensor"] == 2
    return jax.shard_map(
        body if fits else plain_body,
        mesh=mesh,
        in_specs=(
            P("member", "tensor"),
            P("tensor", "member"),
            P("member", "tensor"),
            P("tensor", "member"),
            P(),
        ),
        out_specs=(P("tensor", "member"), P("tensor", "member")),
        check_vma=False,
    )
```

```python
import functools

import jax
import jax.numpy as jnp
from jax import lax
from jax.experimental import pallas as pl
from jax.experimental.pallas import tpu as pltpu
from jax.sharding import PartitionSpec as P

D = 5120
RANK = 4
MEMBER_TOKENS = 16
MESH = pl.DeviceIdType.MESH
NT = (((1,), (1,)), ((), ()))
TN = (((0,), (0,)), ((), ()))


def plain_body(tokens, up_weight, left_factors, right_factors, fitness):
    noise_scale = 0.25 * D ** (-0.5)
    mixing = noise_scale * RANK ** (-0.5)
    width = tokens.shape[1]
    columns = up_weight.shape[1]
    right_all = lax.all_gather(right_factors, "tensor", axis=0, tiled=True)
    members = right_all.shape[0] // RANK
    left_all = lax.all_gather(left_factors, "member", axis=0, tiled=True)
    all_tokens = lax.all_gather(tokens, "member", axis=0, tiled=True)
    projection = jnp.einsum(
        "uzg,uig->uzi",
        all_tokens.reshape(members, MEMBER_TOKENS, width),
        left_all.reshape(members, RANK, width),
        preferred_element_type=jnp.float32,
    ).astype(jnp.bfloat16)
    base = jnp.dot(all_tokens, up_weight, preferred_element_type=jnp.float32)
    correction = jnp.einsum(
        "djt,dty->djy",
        projection,
        right_all.reshape(members, RANK, columns),
        preferred_element_type=jnp.float32,
    ).reshape(base.shape)
    summed = lax.psum_scatter(
        (base + mixing * correction).astype(jnp.bfloat16), "tensor", scatter_dimension=0, tiled=True
    )
    fit_rows = jnp.repeat(fitness, RANK)
    weighted = (fit_rows[:, None] * left_all.astype(jnp.float32)).astype(jnp.bfloat16)
    gradient = jnp.einsum("kd,kf->df", weighted, right_all, preferred_element_type=jnp.float32)
    gradient = gradient * (1.0 / (members * noise_scale * RANK**0.5))
    return (summed, gradient.astype(jnp.bfloat16))


def mirror(step):
    turn = str.maketrans("uv", "vu")
    return [(k, 3 - l, p, dirs.translate(turn)) for k, l, p, dirs in step]


END = [
    [
        ("x", 0, 0, "y"), ("y", 0, 1, "x"), ("c", 1, 0, "xy"), ("c", 1, 1, "xy"),
        ("d", 0, 0, "u"), ("d", 0, 1, "u"),
    ],
    [
        ("c", 2, 0, "xy"), ("c", 2, 1, "xy"), ("c", 3, 0, "xy"),
        ("x", 2, 0, "y"), ("y", 2, 1, "x"), ("c", 3, 1, "xy"),
    ],
    [],
    [],
]
MID = [
    [
        ("c", 2, 0, "v"), ("c", 0, 0, "u"), ("x", 1, 0, "y"), ("y", 1, 1, "x"),
        ("c", 0, 0, "xy"), ("c", 2, 1, "v"), ("c", 0, 1, "u"), ("c", 0, 1, "xy"),
        ("c", 2, 0, "xy"), ("c", 2, 1, "xy"), ("c", 3, 0, "v"),
    ],
    [
        ("c", 3, 1, "v"), ("d", 1, 0, "v"), ("d", 1, 1, "v"),
        ("d", 0, 0, "u"), ("d", 0, 1, "u"),
    ],
    [
        ("x", 2, 0, "y"), ("c", 3, 0, "xy"), ("d", 3, 0, "v"), ("y", 2, 1, "x"),
        ("c", 3, 1, "xy"), ("d", 3, 1, "v"),
    ],
    [],
]
PLAN = [END, MID, [mirror(s) for s in MID], [mirror(s) for s in END]]
ORDER = [[0, 1, 2, 3], [1, 0, 2, 3], [2, 3, 1, 0], [3, 2, 1, 0]]


def tile_of(n, step, most):
    best = step
    for size in range(step, most + 1, step):
        if n % size == 0:
            best = size
    return best


def gather_kernel(
    mixing, tok_in, w_in, left_in, right_in,
    rt_ref, lpad_ref, own_ref, got_ref,
    tok, left, w, rall, sendb,
    send_sem, recv_sem, local_sem, w_sem, r_send, r_recv, p_send, p_recv,
):
    m = lax.axis_index("member")
    t = lax.axis_index("tensor")
    z, y, x = m // 4, (m // 2) % 2, m % 2
    width = tok_in.shape[1]
    half = width // 2
    rows = tok_in.shape[0]
    pad = lpad_ref.shape[0] // 16
    facts = left_in.shape[0]
    ftotal = w.shape[0]

    def at(l, yy, xx):
        return 4 * l + 2 * yy + xx

    def member_of(kind, l):
        if kind == "c":
            return at(l, y, x)
        if kind == "x":
            return at(l, y, 1 - x)
        if kind == "y":
            return at(l, 1 - y, x)
        return at(l, 1 - y, 1 - x)

    barrier = pltpu.get_barrier_semaphore()
    for peer in (at(z, y, 1 - x), at(z, 1 - y, x)):
        pl.semaphore_signal(barrier, inc=1, device_id=(peer, t), device_id_type=MESH)
    pl.semaphore_signal(barrier, inc=1, device_id=(m, 1 - t), device_id_type=MESH)

    @pl.when(z > 0)
    def _():
        pl.semaphore_signal(barrier, inc=1, device_id=(m - 4, t), device_id_type=MESH)

    @pl.when(z < 3)
    def _():
        pl.semaphore_signal(barrier, inc=1, device_id=(m + 4, t), device_id_type=MESH)

    local = [
        pltpu.make_async_copy(tok_in, tok.at[m], local_sem.at[0]),
        pltpu.make_async_copy(left_in, left.at[m], local_sem.at[1]),
        pltpu.make_async_copy(right_in, rall.at[t], local_sem.at[2]),
        pltpu.make_async_copy(w_in, w, w_sem),
    ]
    for copy in local:
        copy.start()

    @pl.when((z == 0) | (z == 3))
    def _():
        pl.semaphore_wait(barrier, 4)

    @pl.when((z == 1) | (z == 2))
    def _():
        pl.semaphore_wait(barrier, 5)

    bufs = (tok, left)

    def peer_of(direction, plane):
        if direction == "x":
            return at(plane, y, 1 - x)
        if direction == "y":
            return at(plane, 1 - y, x)
        return at(plane + (1 if direction == "u" else -1), y, x)

    def copies(event, plane, slot):
        kind, l, part, direction = event
        who = member_of(kind, l)
        span = pl.ds(part * half, half)
        return [
            pltpu.make_async_remote_copy(
                src_ref=((tok_in, left_in)[b] if kind == "c" and l == plane else buf.at[who]).at[:, span],
                dst_ref=buf.at[who].at[:, span],
                send_sem=send_sem.at[b, slot],
                recv_sem=recv_sem.at[b, who, part],
                device_id=(peer_of(direction, plane), t),
                device_id_type=MESH,
            )
            for b, buf in enumerate(bufs)
        ]

    started = {k: [] for k in range(4)}
    waited = {k: set() for k in range(4)}

    def arrive(plane, kind, l, part):
        if (kind, l) == ("c", plane) or (kind, l, part) in waited[plane]:
            return
        waited[plane].add((kind, l, part))
        who = member_of(kind, l)
        for b, buf in enumerate(bufs):
            piece = buf.at[who].at[:, pl.ds(part * half, half)]
            pltpu.make_async_copy(piece, piece, recv_sem.at[b, who, part]).wait()

    def send(event, plane):
        pair = copies(event, plane, len(started[plane]))
        started[plane].append(event)
        for copy in pair:
            copy.start()

    for plane in range(4):
        @pl.when(z == plane)
        def _(plane=plane):
            for nth in range(2):
                for d in {0: "xyu", 3: "xyv"}.get(plane, "uvxy"):
                    send(("c", plane, 1 - nth if d == "y" else nth, d), plane)

    r_copy = pltpu.make_async_remote_copy(
        src_ref=right_in, dst_ref=rall.at[t], send_sem=r_send, recv_sem=r_recv,
        device_id=(m, 1 - t), device_id_type=MESH,
    )
    r_copy.start()

    lpad_ref[...] = jnp.zeros_like(lpad_ref)
    kk = lax.broadcasted_iota(jnp.int32, (2 * rall.shape[1], 16 * pad), 0)
    qq = lax.broadcasted_iota(jnp.int32, (2 * rall.shape[1], 16 * pad), 1)
    slot_q = qq % pad
    spread = jnp.where((slot_q < facts) & (kk == facts * (qq // pad) + slot_q), 1.0, 0.0)
    spread = spread.astype(jnp.bfloat16)
    local[2].wait()
    r_copy.wait()
    r_val = jnp.concatenate([rall[0], rall[1]], axis=0)
    rt_ref[...] = lax.dot_general(
        r_val, spread, TN, preferred_element_type=jnp.float32
    ).astype(jnp.bfloat16)
    local[0].wait()
    local[1].wait()

    ft = tile_of(ftotal, 16, 448)
    tiles = ftotal // ft
    pieces = p_send.shape[1] if tiles % p_send.shape[1] == 0 else 1

    def layer_index(step):
        ind = 0
        for plane in range(4):
            ind = ind + jnp.where(z == plane, ORDER[plane][step], 0)
        return ind

    def compute(l):
        side = l % 2
        for i in range(4):
            lv = left[4 * l + i]
            if facts < pad:
                lv = jnp.concatenate([lv, jnp.zeros((pad - facts, width), lv.dtype)], axis=0)
            lpad_ref[pl.ds(pl.multiple_of((4 * l + i) * pad, 16), pad), :] = lv
        toks = tok[pl.ds(4 * l, 4)].reshape(4 * rows, width)
        proj = lax.dot_general(toks, lpad_ref[...], NT, preferred_element_type=jnp.float32)
        rr = lax.broadcasted_iota(jnp.int32, proj.shape, 0)
        qc = lax.broadcasted_iota(jnp.int32, proj.shape, 1)
        sq = qc % pad
        mine = (sq < facts) & (
            (facts // RANK) * (qc // pad) + sq // RANK == (4 * rows // MEMBER_TOKENS) * l + rr // MEMBER_TOKENS
        )
        proj = jnp.where(mine, proj, 0.0).astype(jnp.bfloat16)

        mine_here = l // 2 == t
        for piece in range(pieces):
            @pl.loop(piece * (tiles // pieces), (piece + 1) * (tiles // pieces))
            def _(i):
                span = pl.ds(pl.multiple_of(i * ft, 16), ft)
                value = lax.dot_general(
                    w[span, :], tok[pl.ds(4 * l, 4)].reshape(4 * rows, width), NT,
                    preferred_element_type=jnp.float32,
                )
                value = value + mixing * lax.dot_general(
                    rt_ref[span, :], proj, NT, preferred_element_type=jnp.float32
                )
                value = value.astype(jnp.bfloat16)

                @pl.when(mine_here)
                def _():
                    own_ref[side, span, :] = value

                @pl.when(jnp.logical_not(mine_here))
                def _():
                    sendb[side, span, :] = value

            @pl.when(jnp.logical_not(mine_here))
            def _():
                exchange(side, piece).start()

    def exchange(side, piece):
        span = pl.ds(piece * (ftotal // pieces), ftotal // pieces)
        return pltpu.make_async_remote_copy(
            src_ref=sendb.at[side].at[span], dst_ref=got_ref.at[side].at[span],
            send_sem=p_send.at[side, piece], recv_sem=p_recv.at[side, piece],
            device_id=(m, 1 - t), device_id_type=MESH,
        )

    for step in range(4):
        for plane in range(4):
            @pl.when(z == plane)
            def _(plane=plane, step=step):
                for kind, l, part, dirs in PLAN[plane][step]:
                    arrive(plane, kind, l, part)
                    for d in dirs:
                        send((kind, l, part, d), plane)
                for kind in "cxyd":
                    for part in range(2):
                        arrive(plane, kind, ORDER[plane][step], part)
        if step == 0:
            local[3].wait()
        compute(layer_index(step))

    for plane in range(4):
        @pl.when(z == plane)
        def _(plane=plane):
            for slot, event in enumerate(started[plane]):
                for copy in copies(event, plane, slot):
                    copy.wait_send()
    for side in range(2):
        for piece in range(pieces):
            exchange(side, piece).wait()


def finish_kernel(scale, facts, fsteps, fit_ref, lpad_ref, rt_ref, own_ref, got_ref, h_ref, g_ref, wl):
    pad = lpad_ref.shape[0] // 16
    i, j = pl.program_id(0), pl.program_id(1)
    tf, td = g_ref.shape

    @pl.when(j == 0)
    def _():
        rows = lax.broadcasted_iota(jnp.int32, (pad, 1), 0) // RANK
        span = pl.ds(pl.multiple_of(i * td, 128), td)
        for b in range(16):
            col = jnp.zeros((pad, 1), jnp.float32)
            for r in range(facts // RANK):
                col = jnp.where(rows == r, fit_ref[b * (facts // RANK) + r], col)
            part = lpad_ref[pl.ds(b * pad, pad), span].astype(jnp.float32) * col
            wl[pl.ds(b * pad, pad), :] = part.astype(jnp.bfloat16)

    fspan = pl.ds(pl.multiple_of(j * tf, 16), tf)
    g = jnp.dot(rt_ref[fspan, :], wl[...], preferred_element_type=jnp.float32)
    g_ref[...] = (g * scale).astype(jnp.bfloat16)
    n = own_ref.shape[2]
    th = h_ref.shape[0]
    at = jnp.minimum(i * pl.num_programs(1) + j, fsteps - 1)
    hspan = pl.ds(pl.multiple_of(at * th, 16), th)
    for side in range(2):
        total = own_ref[side, hspan, :].astype(jnp.float32) + got_ref[side, hspan, :].astype(jnp.float32)
        h_ref[:, side * n:(side + 1) * n] = total.astype(jnp.bfloat16)


def body(tokens, up_weight, left_factors, right_factors, fitness):
    noise_scale = 0.25 * D ** (-0.5)
    mixing = noise_scale * RANK ** (-0.5)
    rows, width = tokens.shape
    facts = left_factors.shape[0]
    columns = up_weight.shape[1]
    rrows = right_factors.shape[0]
    pad = -(-facts // 16) * 16
    members = fitness.shape[0]
    bf = jnp.bfloat16
    anyspec = pl.BlockSpec(memory_space=pltpu.HBM)
    vm = pl.BlockSpec(memory_space=pltpu.VMEM)
    dma = pltpu.SemaphoreType.DMA
    nsend = 40
    part = jax.ShapeDtypeStruct((2, columns, 4 * rows), bf)
    rt, lpad, own, got = pl.pallas_call(
        functools.partial(gather_kernel, mixing),
        out_shape=(
            jax.ShapeDtypeStruct((columns, 16 * pad), bf),
            jax.ShapeDtypeStruct((16 * pad, width), bf),
            part,
            part,
        ),
        in_specs=[anyspec] * 4,
        out_specs=(vm, vm, vm, vm),
        scratch_shapes=[
            pltpu.VMEM((16, rows, width), bf),
            pltpu.VMEM((16, facts, width), bf),
            pltpu.VMEM((columns, width), bf),
            pltpu.VMEM((2, rrows, columns), bf),
            pltpu.VMEM((2, columns, 4 * rows), bf),
            dma((2, nsend)), dma((2, 16, 2)), dma((3,)), dma, dma, dma, dma((2, 2)), dma((2, 2)),
        ],
        compiler_params=pltpu.CompilerParams(
            collective_id=0, has_side_effects=True, vmem_limit_bytes=40 * 1024 * 1024
        ),
        name="gather_project",
    )(
        pltpu.with_memory_space_constraint(tokens, pltpu.HBM),
        pltpu.with_memory_space_constraint(up_weight.T, pltpu.HBM),
        pltpu.with_memory_space_constraint(left_factors, pltpu.HBM),
        pltpu.with_memory_space_constraint(right_factors, pltpu.HBM),
    )

    tf = tile_of(columns, 16, 1024)
    td = tile_of(width, 128, 512)
    dsteps, fsteps = width // td, columns // tf
    th = columns
    for size in range(16, columns, 16):
        if columns % size == 0 and columns // size <= dsteps * fsteps:
            th = size
            break
    last = columns // th - 1
    hidden, gradient = pl.pallas_call(
        functools.partial(finish_kernel, 1.0 / (members * noise_scale * RANK**0.5), facts, last + 1),
        grid=(dsteps, fsteps),
        out_shape=(
            jax.ShapeDtypeStruct((columns, 8 * rows), bf),
            jax.ShapeDtypeStruct((columns, width), bf),
        ),
        in_specs=[pl.BlockSpec(memory_space=pltpu.SMEM), vm, vm, vm, vm],
        out_specs=(
            pl.BlockSpec((th, 8 * rows), lambda i, j: (jnp.minimum(i * fsteps + j, last), 0)),
            pl.BlockSpec((tf, td), lambda i, j: (j, i)),
        ),
        scratch_shapes=[pltpu.VMEM((16 * pad, td), bf)],
        compiler_params=pltpu.CompilerParams(vmem_limit_bytes=24 * 1024 * 1024),
        name="finish",
    )(fitness, lpad, rt, own, got)
    return hidden.T, gradient.T


def solution(mesh):
    fits = mesh.shape["member"] == 16 and mesh.shape["tensor"] == 2
    return jax.shard_map(
        body if fits else plain_body,
        mesh=mesh,
        in_specs=(
            P("member", "tensor"),
            P("tensor", "member"),
            P("member", "tensor"),
            P("tensor", "member"),
            P(),
        ),
        out_specs=(P("tensor", "member"), P("tensor", "member")),
        check_vma=False,
    )
```

```python
import functools

import jax
import jax.numpy as jnp
from jax import lax
from jax.experimental import pallas as pl
from jax.experimental.pallas import tpu as pltpu
from jax.sharding import PartitionSpec as P

D = 5120
RANK = 4
MEMBER_TOKENS = 16
MESH = pl.DeviceIdType.MESH
NT = (((1,), (1,)), ((), ()))
TN = (((0,), (0,)), ((), ()))


def plain_body(tokens, up_weight, left_factors, right_factors, fitness):
    noise_scale = 0.25 * D ** (-0.5)
    mixing = noise_scale * RANK ** (-0.5)
    width = tokens.shape[1]
    columns = up_weight.shape[1]
    right_all = lax.all_gather(right_factors, "tensor", axis=0, tiled=True)
    members = right_all.shape[0] // RANK
    left_all = lax.all_gather(left_factors, "member", axis=0, tiled=True)
    all_tokens = lax.all_gather(tokens, "member", axis=0, tiled=True)
    projection = jnp.einsum(
        "uzg,uig->uzi",
        all_tokens.reshape(members, MEMBER_TOKENS, width),
        left_all.reshape(members, RANK, width),
        preferred_element_type=jnp.float32,
    ).astype(jnp.bfloat16)
    base = jnp.dot(all_tokens, up_weight, preferred_element_type=jnp.float32)
    correction = jnp.einsum(
        "djt,dty->djy",
        projection,
        right_all.reshape(members, RANK, columns),
        preferred_element_type=jnp.float32,
    ).reshape(base.shape)
    summed = lax.psum_scatter(
        (base + mixing * correction).astype(jnp.bfloat16), "tensor", scatter_dimension=0, tiled=True
    )
    fit_rows = jnp.repeat(fitness, RANK)
    weighted = (fit_rows[:, None] * left_all.astype(jnp.float32)).astype(jnp.bfloat16)
    gradient = jnp.einsum("kd,kf->df", weighted, right_all, preferred_element_type=jnp.float32)
    gradient = gradient * (1.0 / (members * noise_scale * RANK**0.5))
    return (summed, gradient.astype(jnp.bfloat16))


def mirror(step):
    turn = str.maketrans("uv", "vu")
    return [(k, 3 - l, p, dirs.translate(turn)) for k, l, p, dirs in step]


END = [
    [
        ("x", 0, 0, "y"), ("y", 0, 1, "x"), ("c", 1, 0, "xy"), ("c", 1, 1, "xy"),
        ("d", 0, 0, "u"), ("d", 0, 1, "u"),
    ],
    [
        ("c", 2, 0, "xy"), ("c", 2, 1, "xy"), ("c", 3, 0, "xy"),
        ("x", 2, 0, "y"), ("y", 2, 1, "x"), ("c", 3, 1, "xy"),
    ],
    [],
    [],
]
MID = [
    [
        ("c", 2, 0, "v"), ("c", 0, 0, "u"), ("x", 1, 0, "y"), ("y", 1, 1, "x"),
        ("c", 0, 0, "xy"), ("c", 2, 1, "v"), ("c", 0, 1, "u"), ("c", 0, 1, "xy"),
        ("c", 2, 0, "xy"), ("c", 2, 1, "xy"), ("c", 3, 0, "v"),
    ],
    [
        ("c", 3, 1, "v"), ("d", 1, 0, "v"), ("d", 1, 1, "v"),
        ("d", 0, 0, "u"), ("d", 0, 1, "u"),
    ],
    [
        ("x", 2, 0, "y"), ("c", 3, 0, "xy"), ("d", 3, 0, "v"), ("y", 2, 1, "x"),
        ("c", 3, 1, "xy"), ("d", 3, 1, "v"),
    ],
    [],
]
PLAN = [END, MID, [mirror(s) for s in MID], [mirror(s) for s in END]]
ORDER = [[0, 1, 2, 3], [1, 0, 2, 3], [2, 3, 1, 0], [3, 2, 1, 0]]


def tile_of(n, step, most):
    best = step
    for size in range(step, most + 1, step):
        if n % size == 0:
            best = size
    return best


def gather_kernel(
    mixing, tok_in, w_in, left_in, right_in,
    rt_ref, lpad_ref, own_ref, got_ref,
    tok, left, w, rall, sendb,
    send_sem, recv_sem, local_sem, w_sem, r_send, r_recv, p_send, p_recv,
):
    m = lax.axis_index("member")
    t = lax.axis_index("tensor")
    z, y, x = m // 4, (m // 2) % 2, m % 2
    width = tok_in.shape[1]
    half = width // 2
    rows = tok_in.shape[0]
    pad = lpad_ref.shape[0] // 16
    facts = left_in.shape[0]
    ftotal = w.shape[0]

    def at(l, yy, xx):
        return 4 * l + 2 * yy + xx

    def member_of(kind, l):
        if kind == "c":
            return at(l, y, x)
        if kind == "x":
            return at(l, y, 1 - x)
        if kind == "y":
            return at(l, 1 - y, x)
        return at(l, 1 - y, 1 - x)

    barrier = pltpu.get_barrier_semaphore()
    for peer in (at(z, y, 1 - x), at(z, 1 - y, x)):
        pl.semaphore_signal(barrier, inc=1, device_id=(peer, t), device_id_type=MESH)
    pl.semaphore_signal(barrier, inc=1, device_id=(m, 1 - t), device_id_type=MESH)

    @pl.when(z > 0)
    def _():
        pl.semaphore_signal(barrier, inc=1, device_id=(m - 4, t), device_id_type=MESH)

    @pl.when(z < 3)
    def _():
        pl.semaphore_signal(barrier, inc=1, device_id=(m + 4, t), device_id_type=MESH)

    local = [
        pltpu.make_async_copy(tok_in, tok.at[m], local_sem.at[0]),
        pltpu.make_async_copy(left_in, left.at[m], local_sem.at[1]),
        pltpu.make_async_copy(right_in, rall.at[t], local_sem.at[2]),
        pltpu.make_async_copy(w_in, w, w_sem),
    ]
    for copy in local:
        copy.start()

    @pl.when((z == 0) | (z == 3))
    def _():
        pl.semaphore_wait(barrier, 4)

    @pl.when((z == 1) | (z == 2))
    def _():
        pl.semaphore_wait(barrier, 5)

    bufs = (tok, left)

    def peer_of(direction, plane):
        if direction == "x":
            return at(plane, y, 1 - x)
        if direction == "y":
            return at(plane, 1 - y, x)
        return at(plane + (1 if direction == "u" else -1), y, x)

    def copies(event, plane, slot):
        kind, l, part, direction = event
        who = member_of(kind, l)
        span = pl.ds(part * half, half)
        return [
            pltpu.make_async_remote_copy(
                src_ref=((tok_in, left_in)[b] if kind == "c" and l == plane else buf.at[who]).at[:, span],
                dst_ref=buf.at[who].at[:, span],
                send_sem=send_sem.at[b, slot],
                recv_sem=recv_sem.at[b, who, part],
                device_id=(peer_of(direction, plane), t),
                device_id_type=MESH,
            )
            for b, buf in enumerate(bufs)
        ]

    started = {k: [] for k in range(4)}
    waited = {k: set() for k in range(4)}

    def arrive(plane, kind, l, part):
        if (kind, l) == ("c", plane) or (kind, l, part) in waited[plane]:
            return
        waited[plane].add((kind, l, part))
        who = member_of(kind, l)
        for b, buf in enumerate(bufs):
            piece = buf.at[who].at[:, pl.ds(part * half, half)]
            pltpu.make_async_copy(piece, piece, recv_sem.at[b, who, part]).wait()

    def send(event, plane):
        pair = copies(event, plane, len(started[plane]))
        started[plane].append(event)
        for copy in pair:
            copy.start()

    for plane in range(4):
        @pl.when(z == plane)
        def _(plane=plane):
            for nth in range(2):
                for d in {0: "xyu", 3: "xyv"}.get(plane, "uvxy"):
                    send(("c", plane, 1 - nth if d == "y" else nth, d), plane)

    r_copy = pltpu.make_async_remote_copy(
        src_ref=right_in, dst_ref=rall.at[t], send_sem=r_send, recv_sem=r_recv,
        device_id=(m, 1 - t), device_id_type=MESH,
    )
    r_copy.start()

    lpad_ref[...] = jnp.zeros_like(lpad_ref)
    kk = lax.broadcasted_iota(jnp.int32, (2 * rall.shape[1], 16 * pad), 0)
    qq = lax.broadcasted_iota(jnp.int32, (2 * rall.shape[1], 16 * pad), 1)
    slot_q = qq % pad
    spread = jnp.where((slot_q < facts) & (kk == facts * (qq // pad) + slot_q), 1.0, 0.0)
    spread = spread.astype(jnp.bfloat16)
    local[2].wait()
    r_copy.wait()
    r_val = jnp.concatenate([rall[0], rall[1]], axis=0)
    rt_ref[...] = lax.dot_general(
        r_val, spread, TN, preferred_element_type=jnp.float32
    ).astype(jnp.bfloat16)
    local[0].wait()
    local[1].wait()

    ft = tile_of(ftotal, 16, 448)
    tiles = ftotal // ft
    pieces = p_send.shape[1] if tiles % p_send.shape[1] == 0 else 1

    def layer_index(step):
        ind = 0
        for plane in range(4):
            ind = ind + jnp.where(z == plane, ORDER[plane][step], 0)
        return ind

    def compute(l):
        side = l % 2
        for i in range(4):
            lv = left[4 * l + i]
            if facts < pad:
                lv = jnp.concatenate([lv, jnp.zeros((pad - facts, width), lv.dtype)], axis=0)
            lpad_ref[pl.ds(pl.multiple_of((4 * l + i) * pad, 16), pad), :] = lv
        toks = tok[pl.ds(4 * l, 4)].reshape(4 * rows, width)
        proj = lax.dot_general(toks, lpad_ref[...], NT, preferred_element_type=jnp.float32)
        rr = lax.broadcasted_iota(jnp.int32, proj.shape, 0)
        qc = lax.broadcasted_iota(jnp.int32, proj.shape, 1)
        sq = qc % pad
        mine = (sq < facts) & (
            (facts // RANK) * (qc // pad) + sq // RANK == (4 * rows // MEMBER_TOKENS) * l + rr // MEMBER_TOKENS
        )
        proj = jnp.where(mine, proj, 0.0).astype(jnp.bfloat16)

        mine_here = l // 2 == t
        for piece in range(pieces):
            @pl.loop(piece * (tiles // pieces), (piece + 1) * (tiles // pieces))
            def _(i):
                span = pl.ds(pl.multiple_of(i * ft, 16), ft)
                value = lax.dot_general(
                    w[span, :], tok[pl.ds(4 * l, 4)].reshape(4 * rows, width), NT,
                    preferred_element_type=jnp.float32,
                )
                value = value + mixing * lax.dot_general(
                    rt_ref[span, :], proj, NT, preferred_element_type=jnp.float32
                )
                value = value.astype(jnp.bfloat16)

                @pl.when(mine_here)
                def _():
                    own_ref[side, span, :] = value

                @pl.when(jnp.logical_not(mine_here))
                def _():
                    sendb[side, span, :] = value

            @pl.when(jnp.logical_not(mine_here))
            def _():
                exchange(side, piece).start()

    def exchange(side, piece):
        span = pl.ds(piece * (ftotal // pieces), ftotal // pieces)
        return pltpu.make_async_remote_copy(
            src_ref=sendb.at[side].at[span], dst_ref=got_ref.at[side].at[span],
            send_sem=p_send.at[side, piece], recv_sem=p_recv.at[side, piece],
            device_id=(m, 1 - t), device_id_type=MESH,
        )

    for step in range(4):
        for plane in range(4):
            @pl.when(z == plane)
            def _(plane=plane, step=step):
                for kind, l, part, dirs in PLAN[plane][step]:
                    arrive(plane, kind, l, part)
                    for d in dirs:
                        send((kind, l, part, d), plane)
                for kind in "cxyd":
                    for part in range(2):
                        arrive(plane, kind, ORDER[plane][step], part)
        if step == 0:
            local[3].wait()
        compute(layer_index(step))

    for plane in range(4):
        @pl.when(z == plane)
        def _(plane=plane):
            for slot, event in enumerate(started[plane]):
                for copy in copies(event, plane, slot):
                    copy.wait_send()
    for side in range(2):
        for piece in range(pieces):
            exchange(side, piece).wait()


def finish_kernel(
    scale, facts, tf, td, th, fit_ref, lpad_ref, rt_ref, own_ref, got_ref,
    h_ref, g_ref, wl, gbuf, hbuf, g_sem, h_sem,
):
    pad = lpad_ref.shape[0] // 16
    columns, width = gbuf.shape
    n = own_ref.shape[2]
    rows = lax.broadcasted_iota(jnp.int32, (pad, 1), 0) // RANK
    copies = []
    slices = columns // th
    for i in range(width // td):
        span = pl.ds(i * td, td)
        for b in range(16):
            col = jnp.zeros((pad, 1), jnp.float32)
            for r in range(facts // RANK):
                col = jnp.where(rows == r, fit_ref[b * (facts // RANK) + r], col)
            part = lpad_ref[pl.ds(b * pad, pad), span].astype(jnp.float32) * col
            wl[pl.ds(b * pad, pad), span] = part.astype(jnp.bfloat16)
        for j in range(columns // tf):
            nth = i * (columns // tf) + j
            fspan = pl.ds(j * tf, tf)
            g = jnp.dot(rt_ref[fspan, :], wl[:, span], preferred_element_type=jnp.float32)
            gbuf[fspan, span] = (g * scale).astype(jnp.bfloat16)
            copies.append(pltpu.make_async_copy(gbuf.at[fspan, span], g_ref.at[fspan, span], g_sem.at[nth]))
            copies[-1].start()
            if nth < slices:
                hspan = pl.ds(nth * th, th)
                for side in range(2):
                    total = own_ref[side, hspan, :].astype(jnp.float32)
                    total = total + got_ref[side, hspan, :].astype(jnp.float32)
                    hbuf[hspan, side * n:(side + 1) * n] = total.astype(jnp.bfloat16)
                copies.append(pltpu.make_async_copy(hbuf.at[hspan], h_ref.at[hspan], h_sem.at[nth]))
                copies[-1].start()
    for copy in copies:
        copy.wait()


def body(tokens, up_weight, left_factors, right_factors, fitness):
    noise_scale = 0.25 * D ** (-0.5)
    mixing = noise_scale * RANK ** (-0.5)
    rows, width = tokens.shape
    facts = left_factors.shape[0]
    columns = up_weight.shape[1]
    rrows = right_factors.shape[0]
    pad = -(-facts // 16) * 16
    members = fitness.shape[0]
    bf = jnp.bfloat16
    anyspec = pl.BlockSpec(memory_space=pltpu.HBM)
    vm = pl.BlockSpec(memory_space=pltpu.VMEM)
    dma = pltpu.SemaphoreType.DMA
    nsend = 40
    part = jax.ShapeDtypeStruct((2, columns, 4 * rows), bf)
    rt, lpad, own, got = pl.pallas_call(
        functools.partial(gather_kernel, mixing),
        out_shape=(
            jax.ShapeDtypeStruct((columns, 16 * pad), bf),
            jax.ShapeDtypeStruct((16 * pad, width), bf),
            part,
            part,
        ),
        in_specs=[anyspec] * 4,
        out_specs=(vm, vm, vm, vm),
        scratch_shapes=[
            pltpu.VMEM((16, rows, width), bf),
            pltpu.VMEM((16, facts, width), bf),
            pltpu.VMEM((columns, width), bf),
            pltpu.VMEM((2, rrows, columns), bf),
            pltpu.VMEM((2, columns, 4 * rows), bf),
            dma((2, nsend)), dma((2, 16, 2)), dma((3,)), dma, dma, dma, dma((2, 2)), dma((2, 2)),
        ],
        compiler_params=pltpu.CompilerParams(
            collective_id=0, has_side_effects=True, vmem_limit_bytes=40 * 1024 * 1024
        ),
        name="gather_project",
    )(
        pltpu.with_memory_space_constraint(tokens, pltpu.HBM),
        pltpu.with_memory_space_constraint(up_weight.T, pltpu.HBM),
        pltpu.with_memory_space_constraint(left_factors, pltpu.HBM),
        pltpu.with_memory_space_constraint(right_factors, pltpu.HBM),
    )

    tf = tile_of(columns, 16, 448)
    td = tile_of(width, 128, 512)
    tiles = (columns // tf) * (width // td)
    th = columns
    for size in range(16, columns, 16):
        if columns % size == 0 and columns // size <= tiles:
            th = size
            break
    hidden, gradient = pl.pallas_call(
        functools.partial(
            finish_kernel, 1.0 / (members * noise_scale * RANK**0.5), facts, tf, td, th
        ),
        out_shape=(
            jax.ShapeDtypeStruct((columns, 8 * rows), bf),
            jax.ShapeDtypeStruct((columns, width), bf),
        ),
        in_specs=[pl.BlockSpec(memory_space=pltpu.SMEM), vm, vm, vm, vm],
        out_specs=(anyspec, anyspec),
        scratch_shapes=[
            pltpu.VMEM((16 * pad, width), bf),
            pltpu.VMEM((columns, width), bf),
            pltpu.VMEM((columns, 8 * rows), bf),
            dma((tiles,)),
            dma((columns // th,)),
        ],
        compiler_params=pltpu.CompilerParams(vmem_limit_bytes=24 * 1024 * 1024),
        name="finish",
    )(fitness, lpad, rt, own, got)
    return hidden.T, gradient.T


def solution(mesh):
    fits = mesh.shape["member"] == 16 and mesh.shape["tensor"] == 2
    return jax.shard_map(
        body if fits else plain_body,
        mesh=mesh,
        in_specs=(
            P("member", "tensor"),
            P("tensor", "member"),
            P("member", "tensor"),
            P("tensor", "member"),
            P(),
        ),
        out_specs=(P("tensor", "member"), P("tensor", "member")),
        check_vma=False,
    )
```
